32 devices in a mesh: aa: 8 (over z, y), ba: 4 (over x, core).
Axes of the slice: x: 2, y: 2, z: 4, core: 2. Of those that a mesh axis runs over, the one named last changes fastest.
Arguments:
- table_a: bfloat16 [6144, 128], P(('aa', 'ba')), may hold values from -40 to 40
- table_b: bfloat16 [4096, 128], P(('aa', 'ba')), may hold values from -40 to 40
- index_a: int32 [1536], P(('aa', 'ba')), may hold values from 0 to 191
- index_b: int32 [1024], P(('aa', 'ba')), may hold values from 0 to 127
- rotation_prev: bfloat16 [128, 128], replicated, may hold values from -0.5 to 0.5
- column_prior: bfloat16 [1024], P(('aa', 'ba')), may hold values from -8 to 8
Outputs:
- rotation: float32 [128, 128], replicated
- potential_a: float32 [1536], P(('aa', 'ba'))
- potential_b: float32 [1024], P(('aa', 'ba'))
The draws below stay inside these ranges and needn't reach their ends.
Inputs may be any that keep to these rules, and one draw needn't show every extreme that they name: `index_a`: entry r is a node of the block of 192 table rows that starts at row (r // 48) * 192, counted from that block's start. `index_b`: entry r is a node of the block of 128 table rows that starts at row (r // 32) * 128, counted from that block's start.
All inputs are finite; a program needn't handle non-finite values.
Results may differ from the reference program's by a relative error of at most 0.0003.
Values may be sent and summed in bfloat16 or wider, within the bound.
A program may use at most 64 MiB of HBM per device.

```python
import math
import jax
import jax.numpy as jnp
from jax import lax

D = 128
A_DEV = 48
B_DEV = 32
PASSES = 3
NS_ITERS = 8
LOCAL_A = 192
LOCAL_B = 128
NA = 1536
NB = 1024
NODES_A = 6144
NODES_B = 4096


def spread_table(key, rows):
    pieces = jax.random.split(key, 3)
    base = jnp.clip(jax.random.normal(pieces[0], (rows, D), jnp.float32), -4.0, 4.0)
    scale = jnp.exp(jax.random.uniform(pieces[2], (rows, 1), jnp.float32, math.log(0.3), math.log(3.0)))
    data = base * scale
    return jnp.clip(data, -40.0, 40.0).astype(jnp.bfloat16)


def draw_table_a(key, part):
    return spread_table(jax.random.fold_in(key, 101), NODES_A)


def draw_table_b(key, part):
    return spread_table(jax.random.fold_in(key, 202), NODES_B)


def plant(values, stream_key, least, largest):
    longest = values.shape.index(max(values.shape))
    spots = []
    for shift in (0, 1):
        where = [jax.random.randint(jax.random.fold_in(stream_key, axis), (), 0, length) for axis, length in enumerate(values.shape)]
        where[longest] = (where[longest] + shift) % values.shape[longest]
        spots.append(tuple(where))
    return values.at[spots[0]].set(least).at[spots[1]].set(largest)


def block_levels(key, dims, cuts, low, top_value):
    loudness = 1.0
    for axis_at, parts in cuts:
        heights = jax.random.uniform(jax.random.fold_in(jax.random.fold_in(key, 6), axis_at), (parts,), jnp.float32, low / len(cuts), top_value / len(cuts))
        loudness = loudness * jnp.repeat(jnp.exp(heights), dims[axis_at] // parts).reshape((-1,) + (1,) * (len(dims) - 1 - axis_at))
    return loudness


def normal_values(own_key, dims, scale, bound, shards=(), held_as=jnp.bfloat16):
    level = block_levels(own_key, dims, shards, -0.22, 0.18) if shards else 1.0
    array = jax.random.normal(own_key, dims, jnp.float32) * scale * level
    return jnp.minimum(jnp.maximum(array, -bound), bound).astype(held_as)


def setup_inputs(seed: int = 0) -> dict:
    splits = jax.random.split(jax.random.key(seed), 7)
    table_a = draw_table_a(jax.random.fold_in(splits[6], 71), 0)
    table_b = draw_table_b(jax.random.fold_in(splits[6], 71), 0)
    index_a = plant(jax.random.randint(splits[2], (NA,), 0, LOCAL_A), jax.random.fold_in(splits[2], 1), 0, LOCAL_A - 1).astype(jnp.int32)
    index_b = plant(jax.random.randint(splits[3], (NB,), 0, LOCAL_B), jax.random.fold_in(splits[3], 1), 0, LOCAL_B - 1).astype(jnp.int32)
    rotation_prev = normal_values(splits[4], (D, D), D ** -0.5, 0.5)
    column_prior = normal_values(splits[5], (NB,), 2.0, 8.0, ((0, 32),))
    return {"table_a": table_a, "table_b": table_b, "index_a": index_a, "index_b": index_b, "rotation_prev": rotation_prev, "column_prior": column_prior}


SCORE_SCALE = 0.0625

def select_rows(table, index, per_device, local):
    owner = jnp.arange(index.shape[0], dtype=jnp.int32) // per_device
    return jnp.take(table, owner * local + index.astype(jnp.int32), axis=0)

def polar_factor(covariance):
    current = covariance / jnp.sqrt(jnp.sum(covariance * covariance) + 1e-06)
    for sweep in range(NS_ITERS):
        square = jnp.dot(current, current.T, precision=lax.Precision.HIGHEST)
        current = 1.5 * current - 0.5 * jnp.dot(square, current, precision=lax.Precision.HIGHEST)
    return current

def reference(table_a, table_b, index_a, index_b, rotation_prev, column_prior):
    rows_a = select_rows(table_a, index_a, A_DEV, LOCAL_A)
    rows_b = select_rows(table_b, index_b, B_DEV, LOCAL_B)
    prior = column_prior.astype(jnp.float32)
    float_a = rows_a.astype(jnp.float32)
    float_b = rows_b.astype(jnp.float32)
    turned_prev = jnp.dot(rows_b, rotation_prev.T, preferred_element_type=jnp.float32)
    block = math.gcd(NA, 512)
    blocks_a = float_a.reshape(NA // block, block, D)

    def covariance_block(piece):
        logits = jnp.dot(piece, turned_prev.T, precision=lax.Precision.HIGHEST) * SCORE_SCALE + prior[None, :]
        weights = jax.nn.softmax(logits, axis=1)
        mixed = jnp.dot(weights, float_b, precision=lax.Precision.HIGHEST)
        return jnp.dot(piece.T, mixed, precision=lax.Precision.HIGHEST)
    covariance = lax.optimization_barrier(jnp.sum(lax.map(covariance_block, blocks_a), axis=0)) / NA
    rotation = polar_factor(covariance)
    turned = jnp.dot(float_b, rotation.T, precision=lax.Precision.HIGHEST)
    potential_b = prior
    potential_a = jnp.zeros((NA,), jnp.float32)
    for sweep in range(PASSES):

        def row_pass(piece, column_pot=potential_b):
            logits = jnp.dot(piece, turned.T, precision=lax.Precision.HIGHEST) * SCORE_SCALE + column_pot[None, :]
            return -math.log(NA) - jax.nn.logsumexp(logits, axis=1)
        potential_a = lax.map(row_pass, blocks_a).reshape(NA)
        row_blocks = potential_a.reshape(NA // block, block)

        def column_step(carry, items):
            peak, mass = carry
            piece, row_pot = items
            logits = jnp.dot(piece, turned.T, precision=lax.Precision.HIGHEST) * SCORE_SCALE + row_pot[:, None]
            top = jnp.maximum(peak, lax.optimization_barrier(jnp.max(logits, axis=0)))
            mass = mass * jnp.exp(peak - top) + lax.optimization_barrier(jnp.sum(jnp.exp(logits - top[None, :]), axis=0))
            return ((top, mass), None)
        start = (jnp.full((NB,), -jnp.inf, jnp.float32), jnp.zeros((NB,), jnp.float32))
        (peak, mass), unused = lax.scan(column_step, start, (blocks_a, row_blocks))
        potential_b = -math.log(NB) - (peak + jnp.log(mass))
    return (rotation, potential_a, potential_b)
```

```python
import functools
import math

import jax
import jax.numpy as jnp
from jax import lax
from jax.experimental import pallas as pl
from jax.experimental.pallas import tpu as pltpu
from jax.sharding import PartitionSpec as P

PASSES = 3
NS_ITERS = 8


SCORE_SCALE = 0.0625


def combined_all(x, axis, combine):
    everything = jax.tree.map(lambda part: lax.all_gather(part, axis), x)
    initial = jax.tree.map(lambda part: part[0], everything)

    def hop(k, so_far):
        return combine(so_far, jax.tree.map(lambda part: part[k], everything))

    return lax.fori_loop(1, lax.axis_size(axis), hop, initial)


def polar_factor(covariance):
    current = covariance / jnp.sqrt(jnp.sum(covariance * covariance) + 1e-06)
    for sweep in range(NS_ITERS):
        square = jnp.dot(current, current.T, precision=lax.Precision.HIGHEST)
        current = 1.5 * current - 0.5 * jnp.dot(square, current, precision=lax.Precision.HIGHEST)
    return current


def combine_totals(first, second):
    peak = jnp.maximum(first[0], second[0])
    return (peak, first[1] * jnp.exp(first[0] - peak) + second[1] * jnp.exp(second[0] - peak))


def row_totals(logits):
    local_peak = jnp.max(logits, axis=1)
    local_mass = jnp.sum(jnp.exp(logits - local_peak[:, None]), axis=1)
    peak, mass = combined_all((local_peak, local_mass), "ba", combine_totals)
    return (peak, mass)


def column_totals(logits):
    local_peak = jnp.max(logits, axis=0)
    local_mass = jnp.sum(jnp.exp(logits - local_peak[None, :]), axis=0)
    peak, mass = combined_all((local_peak, local_mass), "aa", combine_totals)
    return (peak, mass)


def local_collectives(table_a, table_b, index_a, index_b, rotation_prev, column_prior):
    own_a = jnp.take(table_a, index_a, axis=0)
    own_b = jnp.take(table_b, index_b, axis=0)
    rows_a = lax.all_gather(own_a, "ba", axis=0, tiled=True)
    rows_b, prior_low = (
        lax.all_gather(own_b, "aa", axis=0, tiled=True),
        lax.all_gather(column_prior, "aa", axis=0, tiled=True),
    )
    prior = prior_low.astype(jnp.float32)
    devices_all = lax.axis_size("aa") * lax.axis_size("ba")
    total_a = own_a.shape[0] * devices_all
    total_b = own_b.shape[0] * devices_all
    float_a = rows_a.astype(jnp.float32)
    float_b = rows_b.astype(jnp.float32)
    turned_prev = jnp.dot(rows_b, rotation_prev.T, preferred_element_type=jnp.float32)
    logits = (
        jnp.dot(float_a, turned_prev.T, precision=lax.Precision.HIGHEST) * SCORE_SCALE
        + prior[None, :]
    )
    peak, mass = row_totals(logits)
    weights = jnp.exp(logits - peak[:, None]) / mass[:, None]
    mixed = jnp.dot(weights, float_b, precision=lax.Precision.HIGHEST)
    partial_sum = jnp.dot(float_a.T, mixed, precision=lax.Precision.HIGHEST)
    covariance = lax.psum(partial_sum, ("aa", "ba")) / total_a
    rotation = polar_factor(covariance)
    turned = jnp.dot(float_b, rotation.T, precision=lax.Precision.HIGHEST)
    scores = jnp.dot(float_a, turned.T, precision=lax.Precision.HIGHEST) * SCORE_SCALE
    potential_b = prior
    potential_a = jnp.zeros((rows_a.shape[0],), jnp.float32)
    for sweep in range(PASSES):
        peak, mass = row_totals(scores + potential_b[None, :])
        potential_a = -math.log(total_a) - (peak + jnp.log(mass))
        peak, mass = column_totals(scores + potential_a[:, None])
        potential_b = -math.log(total_b) - (peak + jnp.log(mass))
    start_a = lax.axis_index("ba") * own_a.shape[0]
    start_b = lax.axis_index("aa") * own_b.shape[0]
    return (
        rotation,
        lax.dynamic_slice_in_dim(potential_a, start_a, own_a.shape[0]),
        lax.dynamic_slice_in_dim(potential_b, start_b, own_b.shape[0]),
    )


LANES = 128
PACK = 16
LOG2E = math.log2(math.e)
LN2 = math.log(2.0)
MESH = pl.DeviceIdType.MESH
SCORE_BYTES = 8 * 2**20
NT = (((1,), (1,)), ((), ()))
TN = (((0,), (0,)), ((), ()))


def mm(x, y, dims=(((1,), (0,)), ((), ()))):
    return lax.dot_general(x, y, dims, preferred_element_type=jnp.float32)


def pieces(x, count):
    terms = []
    for k in range(count):
        term = x.astype(jnp.bfloat16)
        terms.append(term)
        if k + 1 < count:
            x = x - term.astype(jnp.float32)
    return terms


def square_product(left, right, dims_right):
    l0, l1 = pieces(left, 2)
    r0, r1 = pieces(right, 2)
    lhs = jnp.concatenate([l0, l1], axis=1)
    if dims_right == 1:
        rhs = jnp.concatenate(
            [jnp.concatenate([r0, r0], axis=1), jnp.concatenate([r1, r1], axis=1)], axis=0
        )
        out = mm(lhs, rhs, NT)
    else:
        rhs = jnp.concatenate(
            [jnp.concatenate([r0, r1], axis=1), jnp.concatenate([r0, r1], axis=1)], axis=0
        )
        out = mm(lhs, rhs)
    n = left.shape[0]
    return out[:, :n] + out[:, n:]


def log2(x):
    return jnp.log(x) * LOG2E


def kernel(na, nb, ad, bd,
           ta_ref, tb_ref, ia_ref, ib_ref, rot_ref, prior_ref,
           rot_out, pa_out, pb_out,
           a_buf, b_buf, s_buf, w_buf, cov_buf, cov2_buf, lse_buf, pa_buf, pb_buf,
           az_s, az_r, bz_s, bz_r, ay_s, ay_r, by_s, by_r, bx_s, bx_r, bc_s, bc_r,
           cx_s, cx_r, cc_s, cc_r, l_s, l_r):
    a = lax.axis_index("aa")
    b = lax.axis_index("ba")
    hz, hx = na // 2, nb // 2
    rank = a * nb + b
    rows = na * ad
    cols = na * nb * bd
    groups = cols // LANES
    per = LANES // bd
    mate_a = a + 1 - 2 * lax.rem(a, 2)
    mate_b = b + 1 - 2 * lax.rem(b, 2)

    def za(base, k):
        return lax.rem(base + 2 * k, na)

    def zb(base, k):
        return lax.rem(base + 2 * k, nb)

    barrier = pltpu.get_barrier_semaphore()
    peers = [(za(a, k), b) for k in range(1, hz)] + [(mate_a, b)]
    peers += [(a, lax.rem(b + k, nb)) for k in range(1, nb)]
    for peer in peers:
        pl.semaphore_signal(barrier, inc=1, device_id=peer, device_id_type=MESH)

    def chosen(index_ref, table_ref):
        table = table_ref[...]
        count = index_ref.shape[1]
        spots = lax.broadcasted_iota(jnp.int32, (table.shape[0], count), 0)
        hot = jnp.where(spots == index_ref[...], 1.0, 0.0).astype(jnp.bfloat16)
        return mm(hot, table, TN).astype(jnp.bfloat16)

    a_buf[a] = chosen(ia_ref, ta_ref)
    own_b = chosen(ib_ref, tb_ref)
    offset = lax.rem(rank, per) * bd
    place = (
        lax.broadcasted_iota(jnp.int32, (bd, LANES), 1)
        == lax.broadcasted_iota(jnp.int32, (bd, LANES), 0) + offset
    )
    placed = mm(
        jnp.broadcast_to(prior_ref[...].astype(jnp.float32), (PACK, bd)).astype(jnp.bfloat16),
        jnp.where(place, 1.0, 0.0).astype(jnp.bfloat16),
    )
    b_buf[rank, 0:bd] = own_b
    b_buf[rank, bd:bd + PACK] = placed.astype(jnp.bfloat16)
    pl.semaphore_wait(barrier, len(peers))

    sent = []

    def send(ref, send_sem, recv_sem, peer):
        copy = pltpu.make_async_remote_copy(
            src_ref=ref, dst_ref=ref, send_sem=send_sem, recv_sem=recv_sem,
            device_id=peer, device_id_type=MESH,
        )
        copy.start()
        sent.append(copy)

    def arrived(ref, send_sem, recv_sem, peer):
        pltpu.make_async_remote_copy(
            src_ref=ref, dst_ref=ref, send_sem=send_sem, recv_sem=recv_sem,
            device_id=peer, device_id_type=MESH,
        ).wait_recv()

    def spread_b(ref, slot):
        for k in range(1, hx):
            where = slot * hx + k
            send(ref, bx_s.at[where], bx_r.at[where], (a, zb(b, k)))
        send(ref, bc_s.at[slot * hx], bc_r.at[slot * hx], (a, mate_b))

    own_a_ref = a_buf.at[a]
    own_b_ref = b_buf.at[rank]
    for k in range(1, hz):
        send(own_b_ref, bz_s.at[k], bz_r.at[k], (za(a, k), b))
    send(own_b_ref, by_s.at[0], by_r.at[0], (mate_a, b))
    for k in range(1, hz):
        send(own_a_ref, az_s.at[k], az_r.at[k], (za(a, k), b))
    spread_b(own_b_ref, 0)
    send(own_a_ref, ay_s.at[0], ay_r.at[0], (mate_a, b))

    for k in range(1, hz):
        origin = za(a, hz - k)
        ref = b_buf.at[origin * nb + b]
        arrived(ref, bz_s.at[k], bz_r.at[k], (origin, b))
        send(ref, by_s.at[k], by_r.at[k], (mate_a, b))
        spread_b(ref, k)
        ref = a_buf.at[origin]
        arrived(ref, az_s.at[k], az_r.at[k], (origin, b))
        send(ref, ay_s.at[k], ay_r.at[k], (mate_a, b))
    for k in range(hz):
        origin = za(mate_a, hz - k)
        ref = b_buf.at[origin * nb + b]
        arrived(ref, by_s.at[k], by_r.at[k], (mate_a, b))
        spread_b(ref, hz + k)
    for k in range(hz):
        origin = za(mate_a, hz - k)
        arrived(a_buf.at[origin], ay_s.at[k], ay_r.at[k], (mate_a, b))

    def slot_origin(slot):
        return za(a, hz - slot) if slot < hz else za(mate_a, 2 * hz - slot)

    for slot in range(na):
        for k in range(1, hx):
            where = slot * hx + k
            from_b = zb(b, hx - k)
            ref = b_buf.at[slot_origin(slot) * nb + from_b]
            arrived(ref, bx_s.at[where], bx_r.at[where], (a, from_b))
            send(ref, bc_s.at[where], bc_r.at[where], (a, mate_b))

    rows_a = a_buf[...].reshape(rows, LANES)
    factor = SCORE_SCALE * LOG2E
    query = mm(rows_a, rot_ref[...]) * factor
    query = jnp.concatenate(pieces(query, 3), axis=1)

    for slot in range(na):
        for k in range(hx):
            where = slot * hx + k
            ref = b_buf.at[slot_origin(slot) * nb + zb(mate_b, hx - k)]
            arrived(ref, bc_s.at[where], bc_r.at[where], (a, mate_b))

    rows_b = b_buf[:, 0:bd, :].reshape(cols, LANES)
    rows_b3 = jnp.concatenate([rows_b] * 3, axis=1)
    for g in range(groups):
        total = b_buf[g * per, bd:bd + PACK].astype(jnp.float32)
        for k in range(1, per):
            total = total + b_buf[g * per + k, bd:bd + PACK].astype(jnp.float32)
        pb_buf[g:g + 1] = total[0:1] * LOG2E

    def group(g):
        return slice(g * LANES, (g + 1) * LANES)

    def row_parts(c, pot):
        here = slice(c * ad, (c + 1) * ad)
        logits = [s_buf[here, group(g)] + pot[g:g + 1] for g in range(groups)]
        peak = jnp.max(functools.reduce(jnp.maximum, logits), axis=1, keepdims=True)
        parts = [jnp.exp2(x - peak) for x in logits]
        mass = jnp.sum(functools.reduce(jnp.add, parts), axis=1, keepdims=True)
        return here, peak, parts, mass

    s_buf[...] = mm(query, rows_b3, NT)
    pot = pb_buf[...]
    for c in range(na):
        here, peak, parts, mass = row_parts(c, pot)
        for g in range(groups):
            high, low = pieces(parts[g], 2)
            w_buf[here, group(g)] = high
            w_buf[here, group(groups + g)] = low
        pa_buf[here] = jnp.broadcast_to(1.0 / mass, (ad, LANES))
    mixed = mm(w_buf[...], jnp.concatenate([rows_b, rows_b], axis=0)) * pa_buf[...]
    both = mm(rows_a, jnp.concatenate(pieces(mixed, 2), axis=1), TN)
    mine = lax.div(b, 2)
    cov_buf[mine] = both[:, :LANES] + both[:, LANES:]
    for k in range(1, hx):
        send(cov_buf.at[mine], cx_s.at[k], cx_r.at[k], (a, zb(b, k)))
    for k in range(1, hx):
        from_b = zb(b, hx - k)
        arrived(cov_buf.at[lax.div(from_b, 2)], cx_s.at[k], cx_r.at[k], (a, from_b))
    side = lax.rem(b, 2)
    cov2_buf[side] = functools.reduce(jnp.add, [cov_buf[k] for k in range(hx)])
    send(cov2_buf.at[side], cc_s, cc_r, (a, mate_b))
    arrived(cov2_buf.at[1 - side], cc_s, cc_r, (a, mate_b))
    current = (cov2_buf[0] + cov2_buf[1]) / (rows * nb)
    norm = jnp.sum(jnp.sum(current * current, axis=1, keepdims=True), axis=0, keepdims=True)
    current = current / jnp.sqrt(norm + 1e-06)
    for sweep in range(NS_ITERS):
        square = square_product(current, current, 1)
        current = 1.5 * current - 0.5 * square_product(square, current, 0)
    rot_out[...] = current

    turn = jnp.concatenate(pieces(current, 3), axis=0)
    query = mm(jnp.concatenate([rows_a] * 3, axis=1), turn) * factor
    query = jnp.concatenate(pieces(query, 3), axis=1)
    s_buf[...] = mm(query, rows_b3, NT)

    for sweep in range(PASSES):
        for c in range(na):
            here, peak, parts, mass = row_parts(c, pot)
            value = -math.log2(rows * nb) - (peak + log2(mass))
            pa_buf[here] = jnp.broadcast_to(value, (ad, LANES))
        for g in range(groups):
            logits = s_buf[:, group(g)] + pa_buf[...]
            peak = jnp.max(logits, axis=0, keepdims=True)
            mass = jnp.sum(jnp.exp2(logits - peak), axis=0, keepdims=True)
            lse_buf[sweep, b, g:g + 1] = peak + log2(mass)
        for k in range(1, nb):
            send(lse_buf.at[sweep, b], l_s.at[sweep, k], l_r.at[sweep, k], (a, lax.rem(b + k, nb)))
        for k in range(1, nb):
            from_b = lax.rem(b + nb - k, nb)
            arrived(lse_buf.at[sweep, from_b], l_s.at[sweep, k], l_r.at[sweep, k], (a, from_b))
        parts = [lse_buf[sweep, k] for k in range(nb)]
        peak = functools.reduce(jnp.maximum, parts)
        mass = functools.reduce(jnp.add, [jnp.exp2(x - peak) for x in parts])
        pot = -math.log2(cols) - (peak + log2(mass))

    def to_row(column, n):
        eye = (
            lax.broadcasted_iota(jnp.int32, (n, n), 0)
            == lax.broadcasted_iota(jnp.int32, (n, n), 1)
        )
        return jnp.sum(jnp.where(eye, column, 0.0), axis=0, keepdims=True)

    own = pa_buf[pl.ds(pl.multiple_of(a * ad, 8), ad), 0:ad]
    pa_out[...] = to_row(own, ad) * LN2
    pb_buf[...] = pot
    line = pb_buf[pl.ds(lax.div(rank, per), 1)]
    column = jnp.sum(
        jnp.where(place, jnp.broadcast_to(line, (bd, LANES)), 0.0), axis=1, keepdims=True
    )
    pb_out[...] = to_row(jnp.broadcast_to(column, (bd, bd)), bd) * LN2
    for copy in sent:
        copy.wait_send()


def local_kernel(na, nb, table_a, table_b, index_a, index_b, rotation_prev, column_prior):
    ad, bd = index_a.shape[0], index_b.shape[0]
    rows, cols = na * ad, na * nb * bd
    groups = cols // LANES
    hz, hx = na // 2, nb // 2
    dma = pltpu.SemaphoreType.DMA
    f32, bf16 = jnp.float32, jnp.bfloat16
    rotation, pa, pb = pl.pallas_call(
        functools.partial(kernel, na, nb, ad, bd),
        out_shape=(
            jax.ShapeDtypeStruct((LANES, LANES), f32),
            jax.ShapeDtypeStruct((1, ad), f32),
            jax.ShapeDtypeStruct((1, bd), f32),
        ),
        in_specs=[pl.BlockSpec(memory_space=pltpu.VMEM)] * 6,
        out_specs=tuple([pl.BlockSpec(memory_space=pltpu.VMEM)] * 3),
        scratch_shapes=[
            pltpu.VMEM((na, ad, LANES), bf16),
            pltpu.VMEM((na * nb, bd + PACK, LANES), bf16),
            pltpu.VMEM((rows, cols), f32),
            pltpu.VMEM((rows, 2 * cols), bf16),
            pltpu.VMEM((hx, LANES, LANES), f32),
            pltpu.VMEM((2, LANES, LANES), f32),
            pltpu.VMEM((PASSES, nb, groups, LANES), f32),
            pltpu.VMEM((rows, LANES), f32),
            pltpu.VMEM((groups, LANES), f32),
            dma((hz,)), dma((hz,)), dma((hz,)), dma((hz,)),
            dma((hz,)), dma((hz,)), dma((hz,)), dma((hz,)),
            dma((na * hx,)), dma((na * hx,)), dma((na * hx,)), dma((na * hx,)),
            dma((hx,)), dma((hx,)), dma, dma,
            dma((PASSES, nb)), dma((PASSES, nb)),
        ],
        compiler_params=pltpu.CompilerParams(collective_id=0, has_side_effects=True),
    )(
        table_a, table_b, index_a.reshape(1, ad), index_b.reshape(1, bd),
        rotation_prev, column_prior.reshape(1, bd),
    )
    return rotation, pa.reshape(ad), pb.reshape(bd)


def local(table_a, table_b, index_a, index_b, rotation_prev, column_prior):
    na, nb = lax.axis_size("aa"), lax.axis_size("ba")
    ad, bd = index_a.shape[0], index_b.shape[0]
    cols = na * nb * bd
    fits = (
        na % 2 == 0 and nb % 2 == 0 and table_a.shape[1] == LANES
        and ad % PACK == 0 and ad <= LANES and bd % PACK == 0 and LANES % bd == 0
        and cols % LANES == 0 and 4 * na * ad * cols <= SCORE_BYTES
    )
    args = (table_a, table_b, index_a, index_b, rotation_prev, column_prior)
    return local_kernel(na, nb, *args) if fits else local_collectives(*args)


def solution(mesh):
    return jax.shard_map(
        local,
        mesh=mesh,
        in_specs=(
            P(("aa", "ba"), None),
            P(("aa", "ba"), None),
            P(("aa", "ba")),
            P(("aa", "ba")),
            P(),
            P(("aa", "ba")),
        ),
        out_specs=(P(), P(("aa", "ba")), P(("aa", "ba"))),
        check_vma=False,
    )
```

```python
import functools
import math

import jax
import jax.numpy as jnp
from jax import lax
from jax.experimental import pallas as pl
from jax.experimental.pallas import tpu as pltpu
from jax.sharding import PartitionSpec as P

PASSES = 3
NS_ITERS = 8


SCORE_SCALE = 0.0625


def combined_all(x, axis, combine):
    everything = jax.tree.map(lambda part: lax.all_gather(part, axis), x)
    initial = jax.tree.map(lambda part: part[0], everything)

    def hop(k, so_far):
        return combine(so_far, jax.tree.map(lambda part: part[k], everything))

    return lax.fori_loop(1, lax.axis_size(axis), hop, initial)


def polar_factor(covariance):
    current = covariance / jnp.sqrt(jnp.sum(covariance * covariance) + 1e-06)
    for sweep in range(NS_ITERS):
        square = jnp.dot(current, current.T, precision=lax.Precision.HIGHEST)
        current = 1.5 * current - 0.5 * jnp.dot(square, current, precision=lax.Precision.HIGHEST)
    return current


def combine_totals(first, second):
    peak = jnp.maximum(first[0], second[0])
    return (peak, first[1] * jnp.exp(first[0] - peak) + second[1] * jnp.exp(second[0] - peak))


def row_totals(logits):
    local_peak = jnp.max(logits, axis=1)
    local_mass = jnp.sum(jnp.exp(logits - local_peak[:, None]), axis=1)
    peak, mass = combined_all((local_peak, local_mass), "ba", combine_totals)
    return (peak, mass)


def column_totals(logits):
    local_peak = jnp.max(logits, axis=0)
    local_mass = jnp.sum(jnp.exp(logits - local_peak[None, :]), axis=0)
    peak, mass = combined_all((local_peak, local_mass), "aa", combine_totals)
    return (peak, mass)


def local_collectives(table_a, table_b, index_a, index_b, rotation_prev, column_prior):
    own_a = jnp.take(table_a, index_a, axis=0)
    own_b = jnp.take(table_b, index_b, axis=0)
    rows_a = lax.all_gather(own_a, "ba", axis=0, tiled=True)
    rows_b, prior_low = (
        lax.all_gather(own_b, "aa", axis=0, tiled=True),
        lax.all_gather(column_prior, "aa", axis=0, tiled=True),
    )
    prior = prior_low.astype(jnp.float32)
    devices_all = lax.axis_size("aa") * lax.axis_size("ba")
    total_a = own_a.shape[0] * devices_all
    total_b = own_b.shape[0] * devices_all
    float_a = rows_a.astype(jnp.float32)
    float_b = rows_b.astype(jnp.float32)
    turned_prev = jnp.dot(rows_b, rotation_prev.T, preferred_element_type=jnp.float32)
    logits = (
        jnp.dot(float_a, turned_prev.T, precision=lax.Precision.HIGHEST) * SCORE_SCALE
        + prior[None, :]
    )
    peak, mass = row_totals(logits)
    weights = jnp.exp(logits - peak[:, None]) / mass[:, None]
    mixed = jnp.dot(weights, float_b, precision=lax.Precision.HIGHEST)
    partial_sum = jnp.dot(float_a.T, mixed, precision=lax.Precision.HIGHEST)
    covariance = lax.psum(partial_sum, ("aa", "ba")) / total_a
    rotation = polar_factor(covariance)
    turned = jnp.dot(float_b, rotation.T, precision=lax.Precision.HIGHEST)
    scores = jnp.dot(float_a, turned.T, precision=lax.Precision.HIGHEST) * SCORE_SCALE
    potential_b = prior
    potential_a = jnp.zeros((rows_a.shape[0],), jnp.float32)
    for sweep in range(PASSES):
        peak, mass = row_totals(scores + potential_b[None, :])
        potential_a = -math.log(total_a) - (peak + jnp.log(mass))
        peak, mass = column_totals(scores + potential_a[:, None])
        potential_b = -math.log(total_b) - (peak + jnp.log(mass))
    start_a = lax.axis_index("ba") * own_a.shape[0]
    start_b = lax.axis_index("aa") * own_b.shape[0]
    return (
        rotation,
        lax.dynamic_slice_in_dim(potential_a, start_a, own_a.shape[0]),
        lax.dynamic_slice_in_dim(potential_b, start_b, own_b.shape[0]),
    )


LANES = 128
PACK = 16
LOG2E = math.log2(math.e)
LN2 = math.log(2.0)
MESH = pl.DeviceIdType.MESH
SCORE_BYTES = 8 * 2**20
NT = (((1,), (1,)), ((), ()))
TN = (((0,), (0,)), ((), ()))


def mm(x, y, dims=(((1,), (0,)), ((), ()))):
    return lax.dot_general(x, y, dims, preferred_element_type=jnp.float32)


def pieces(x, count):
    terms = []
    for k in range(count):
        term = x.astype(jnp.bfloat16)
        terms.append(term)
        if k + 1 < count:
            x = x - term.astype(jnp.float32)
    return terms


def square_product(left, right, dims_right):
    l0, l1 = pieces(left, 2)
    r0, r1 = pieces(right, 2)
    lhs = jnp.concatenate([l0, l1], axis=1)
    if dims_right == 1:
        rhs = jnp.concatenate(
            [jnp.concatenate([r0, r0], axis=1), jnp.concatenate([r1, r1], axis=1)], axis=0
        )
        out = mm(lhs, rhs, NT)
    else:
        rhs = jnp.concatenate(
            [jnp.concatenate([r0, r1], axis=1), jnp.concatenate([r0, r1], axis=1)], axis=0
        )
        out = mm(lhs, rhs)
    n = left.shape[0]
    return out[:, :n] + out[:, n:]


def log2(x):
    return jnp.log(x) * LOG2E


def kernel(na, nb, ad, bd,
           ta_in, tb_in, ia_in, ib_in, rot_in, prior_in,
           rot_out, pa_out, pb_out,
           ta_ref, tb_ref, ia_ref, ib_ref, rot_ref, prior_ref, in_sem,
           a_buf, b_buf, s_buf, w_buf, cov_buf, cov2_buf, lse_buf, pa_buf, pb_buf,
           az_s, az_r, bz_s, bz_r, ay_s, ay_r, by_s, by_r, bx_s, bx_r, bc_s, bc_r,
           cx_s, cx_r, cc_s, cc_r, l_s, l_r):
    a = lax.axis_index("aa")
    b = lax.axis_index("ba")
    hz, hx = na // 2, nb // 2
    rank = a * nb + b
    rows = na * ad
    cols = na * nb * bd
    groups = cols // LANES
    per = LANES // bd
    mate_a = a + 1 - 2 * lax.rem(a, 2)
    mate_b = b + 1 - 2 * lax.rem(b, 2)

    def za(base, k):
        return lax.rem(base + 2 * k, na)

    def zb(base, k):
        return lax.rem(base + 2 * k, nb)

    barrier = pltpu.get_barrier_semaphore()
    peers = [(za(a, k), b) for k in range(1, hz)] + [(mate_a, b)]
    peers += [(a, lax.rem(b + k, nb)) for k in range(1, nb)]
    for peer in peers:
        pl.semaphore_signal(barrier, inc=1, device_id=peer, device_id_type=MESH)

    loads = [
        pltpu.make_async_copy(source, target, in_sem.at[k])
        for k, (source, target) in enumerate((
            (ib_in, ib_ref), (tb_in, tb_ref), (prior_in, prior_ref),
            (ia_in, ia_ref), (ta_in, ta_ref), (rot_in, rot_ref),
        ))
    ]
    for load in loads:
        load.start()
    for load in loads:
        load.wait()

    def chosen(index_ref, table_ref):
        table = table_ref[...]
        count = index_ref.shape[1]
        spots = lax.broadcasted_iota(jnp.int32, (table.shape[0], count), 0)
        hot = jnp.where(spots == index_ref[...], 1.0, 0.0).astype(jnp.bfloat16)
        return mm(hot, table, TN).astype(jnp.bfloat16)

    a_buf[a] = chosen(ia_ref, ta_ref)
    own_b = chosen(ib_ref, tb_ref)
    offset = lax.rem(rank, per) * bd
    place = (
        lax.broadcasted_iota(jnp.int32, (bd, LANES), 1)
        == lax.broadcasted_iota(jnp.int32, (bd, LANES), 0) + offset
    )
    placed = mm(
        jnp.broadcast_to(prior_ref[...].astype(jnp.float32), (PACK, bd)).astype(jnp.bfloat16),
        jnp.where(place, 1.0, 0.0).astype(jnp.bfloat16),
    )
    b_buf[rank, 0:bd] = own_b
    b_buf[rank, bd:bd + PACK] = placed.astype(jnp.bfloat16)
    pl.semaphore_wait(barrier, len(peers))

    sent = []

    def send(ref, send_sem, recv_sem, peer):
        copy = pltpu.make_async_remote_copy(
            src_ref=ref, dst_ref=ref, send_sem=send_sem, recv_sem=recv_sem,
            device_id=peer, device_id_type=MESH,
        )
        copy.start()
        sent.append(copy)

    def arrived(ref, send_sem, recv_sem, peer):
        pltpu.make_async_remote_copy(
            src_ref=ref, dst_ref=ref, send_sem=send_sem, recv_sem=recv_sem,
            device_id=peer, device_id_type=MESH,
        ).wait_recv()

    def spread_b(ref, slot):
        for k in range(1, hx):
            where = slot * hx + k
            send(ref, bx_s.at[where], bx_r.at[where], (a, zb(b, k)))
        send(ref, bc_s.at[slot * hx], bc_r.at[slot * hx], (a, mate_b))

    own_a_ref = a_buf.at[a]
    own_b_ref = b_buf.at[rank]
    for k in range(1, hz):
        send(own_b_ref, bz_s.at[k], bz_r.at[k], (za(a, k), b))
    send(own_b_ref, by_s.at[0], by_r.at[0], (mate_a, b))
    for k in range(1, hz):
        send(own_a_ref, az_s.at[k], az_r.at[k], (za(a, k), b))
    spread_b(own_b_ref, 0)
    send(own_a_ref, ay_s.at[0], ay_r.at[0], (mate_a, b))

    for k in range(1, hz):
        origin = za(a, hz - k)
        ref = b_buf.at[origin * nb + b]
        arrived(ref, bz_s.at[k], bz_r.at[k], (origin, b))
        send(ref, by_s.at[k], by_r.at[k], (mate_a, b))
        spread_b(ref, k)
    for k in range(1, hz):
        origin = za(a, hz - k)
        ref = a_buf.at[origin]
        arrived(ref, az_s.at[k], az_r.at[k], (origin, b))
        send(ref, ay_s.at[k], ay_r.at[k], (mate_a, b))
    for k in range(hz):
        origin = za(mate_a, hz - k)
        ref = b_buf.at[origin * nb + b]
        arrived(ref, by_s.at[k], by_r.at[k], (mate_a, b))
        spread_b(ref, hz + k)
    def slot_origin(slot):
        return za(a, hz - slot) if slot < hz else za(mate_a, 2 * hz - slot)

    for slot in range(na):
        for k in range(1, hx):
            where = slot * hx + k
            from_b = zb(b, hx - k)
            ref = b_buf.at[slot_origin(slot) * nb + from_b]
            arrived(ref, bx_s.at[where], bx_r.at[where], (a, from_b))
            send(ref, bc_s.at[where], bc_r.at[where], (a, mate_b))

    for k in range(hz):
        origin = za(mate_a, hz - k)
        arrived(a_buf.at[origin], ay_s.at[k], ay_r.at[k], (mate_a, b))
    rows_a = a_buf[...].reshape(rows, LANES)
    factor = SCORE_SCALE * LOG2E
    query = mm(rows_a, rot_ref[...]) * factor
    query = jnp.concatenate(pieces(query, 3), axis=1)

    for slot in range(na):
        for k in range(hx):
            where = slot * hx + k
            ref = b_buf.at[slot_origin(slot) * nb + zb(mate_b, hx - k)]
            arrived(ref, bc_s.at[where], bc_r.at[where], (a, mate_b))

    rows_b = b_buf[:, 0:bd, :].reshape(cols, LANES)
    rows_b3 = jnp.concatenate([rows_b] * 3, axis=1)
    for g in range(groups):
        total = b_buf[g * per, bd:bd + PACK].astype(jnp.float32)
        for k in range(1, per):
            total = total + b_buf[g * per + k, bd:bd + PACK].astype(jnp.float32)
        pb_buf[g:g + 1] = total[0:1] * LOG2E

    def group(g):
        return slice(g * LANES, (g + 1) * LANES)

    def row_parts(c, pot):
        here = slice(c * ad, (c + 1) * ad)
        logits = [s_buf[here, group(g)] + pot[g:g + 1] for g in range(groups)]
        peak = jnp.max(functools.reduce(jnp.maximum, logits), axis=1, keepdims=True)
        parts = [jnp.exp2(x - peak) for x in logits]
        mass = jnp.sum(functools.reduce(jnp.add, parts), axis=1, keepdims=True)
        return here, peak, parts, mass

    s_buf[...] = mm(query, rows_b3, NT)
    pot = pb_buf[...]
    for c in range(na):
        here, peak, parts, mass = row_parts(c, pot)
        for g in range(groups):
            high, low = pieces(parts[g], 2)
            w_buf[here, group(g)] = high
            w_buf[here, group(groups + g)] = low
        pa_buf[here] = jnp.broadcast_to(1.0 / mass, (ad, LANES))
    mixed = mm(w_buf[...], jnp.concatenate([rows_b, rows_b], axis=0)) * pa_buf[...]
    both = mm(rows_a, jnp.concatenate(pieces(mixed, 2), axis=1), TN)
    mine = lax.div(b, 2)
    cov_buf[mine] = both[:, :LANES] + both[:, LANES:]
    for k in range(1, hx):
        send(cov_buf.at[mine], cx_s.at[k], cx_r.at[k], (a, zb(b, k)))
    for k in range(1, hx):
        from_b = zb(b, hx - k)
        arrived(cov_buf.at[lax.div(from_b, 2)], cx_s.at[k], cx_r.at[k], (a, from_b))
    side = lax.rem(b, 2)
    cov2_buf[side] = functools.reduce(jnp.add, [cov_buf[k] for k in range(hx)])
    send(cov2_buf.at[side], cc_s, cc_r, (a, mate_b))
    arrived(cov2_buf.at[1 - side], cc_s, cc_r, (a, mate_b))
    current = (cov2_buf[0] + cov2_buf[1]) / (rows * nb)
    norm = jnp.sum(jnp.sum(current * current, axis=1, keepdims=True), axis=0, keepdims=True)
    current = current / jnp.sqrt(norm + 1e-06)
    for sweep in range(NS_ITERS):
        square = square_product(current, current, 1)
        current = 1.5 * current - 0.5 * square_product(square, current, 0)
    rot_out[...] = current

    turn = jnp.concatenate(pieces(current, 3), axis=0)
    query = mm(jnp.concatenate([rows_a] * 3, axis=1), turn) * factor
    query = jnp.concatenate(pieces(query, 3), axis=1)
    s_buf[...] = mm(query, rows_b3, NT)

    for sweep in range(PASSES):
        for c in range(na):
            here, peak, parts, mass = row_parts(c, pot)
            value = -math.log2(rows * nb) - (peak + log2(mass))
            pa_buf[here] = jnp.broadcast_to(value, (ad, LANES))
        for g in range(groups):
            logits = s_buf[:, group(g)] + pa_buf[...]
            peak = jnp.max(logits, axis=0, keepdims=True)
            mass = jnp.sum(jnp.exp2(logits - peak), axis=0, keepdims=True)
            lse_buf[sweep, b, g:g + 1] = peak + log2(mass)
        for k in range(1, nb):
            send(lse_buf.at[sweep, b], l_s.at[sweep, k], l_r.at[sweep, k], (a, lax.rem(b + k, nb)))
        for k in range(1, nb):
            from_b = lax.rem(b + nb - k, nb)
            arrived(lse_buf.at[sweep, from_b], l_s.at[sweep, k], l_r.at[sweep, k], (a, from_b))
        parts = [lse_buf[sweep, k] for k in range(nb)]
        peak = functools.reduce(jnp.maximum, parts)
        mass = functools.reduce(jnp.add, [jnp.exp2(x - peak) for x in parts])
        pot = -math.log2(cols) - (peak + log2(mass))

    def to_row(column, n):
        eye = (
            lax.broadcasted_iota(jnp.int32, (n, n), 0)
            == lax.broadcasted_iota(jnp.int32, (n, n), 1)
        )
        return jnp.sum(jnp.where(eye, column, 0.0), axis=0, keepdims=True)

    own = pa_buf[pl.ds(pl.multiple_of(a * ad, 8), ad), 0:ad]
    pa_out[...] = to_row(own, ad) * LN2
    pb_buf[...] = pot
    line = pb_buf[pl.ds(lax.div(rank, per), 1)]
    column = jnp.sum(
        jnp.where(place, jnp.broadcast_to(line, (bd, LANES)), 0.0), axis=1, keepdims=True
    )
    pb_out[...] = to_row(jnp.broadcast_to(column, (bd, bd)), bd) * LN2
    for copy in sent:
        copy.wait_send()


def finish(rot_ref, pa_ref, pb_ref, rot_out, pa_out, pb_out):
    rot_out[...] = rot_ref[...]
    pa_out[...] = pa_ref[...]
    pb_out[...] = pb_ref[...]


def local_kernel(na, nb, table_a, table_b, index_a, index_b, rotation_prev, column_prior):
    ad, bd = index_a.shape[0], index_b.shape[0]
    rows, cols = na * ad, na * nb * bd
    groups = cols // LANES
    hz, hx = na // 2, nb // 2
    dma = pltpu.SemaphoreType.DMA
    f32, bf16 = jnp.float32, jnp.bfloat16
    rotation, pa, pb = pl.pallas_call(
        functools.partial(kernel, na, nb, ad, bd),
        out_shape=(
            jax.ShapeDtypeStruct((LANES, LANES), f32),
            jax.ShapeDtypeStruct((1, ad), f32),
            jax.ShapeDtypeStruct((1, bd), f32),
        ),
        in_specs=[pl.BlockSpec(memory_space=pl.ANY)] * 6,
        out_specs=tuple([pl.BlockSpec(memory_space=pltpu.VMEM)] * 3),
        scratch_shapes=[
            pltpu.VMEM(table_a.shape, bf16), pltpu.VMEM(table_b.shape, bf16),
            pltpu.VMEM((1, ad), jnp.int32), pltpu.VMEM((1, bd), jnp.int32),
            pltpu.VMEM((LANES, LANES), bf16), pltpu.VMEM((1, bd), bf16), dma((6,)),
            pltpu.VMEM((na, ad, LANES), bf16),
            pltpu.VMEM((na * nb, bd + PACK, LANES), bf16),
            pltpu.VMEM((rows, cols), f32),
            pltpu.VMEM((rows, 2 * cols), bf16),
            pltpu.VMEM((hx, LANES, LANES), f32),
            pltpu.VMEM((2, LANES, LANES), f32),
            pltpu.VMEM((PASSES, nb, groups, LANES), f32),
            pltpu.VMEM((rows, LANES), f32),
            pltpu.VMEM((groups, LANES), f32),
            dma((hz,)), dma((hz,)), dma((hz,)), dma((hz,)),
            dma((hz,)), dma((hz,)), dma((hz,)), dma((hz,)),
            dma((na * hx,)), dma((na * hx,)), dma((na * hx,)), dma((na * hx,)),
            dma((hx,)), dma((hx,)), dma, dma,
            dma((PASSES, nb)), dma((PASSES, nb)),
        ],
        compiler_params=pltpu.CompilerParams(collective_id=0, has_side_effects=True),
    )(
        table_a, table_b, index_a.reshape(1, ad), index_b.reshape(1, bd),
        rotation_prev, column_prior.reshape(1, bd),
    )
    rotation, pa, pb = pl.pallas_call(
        finish,
        out_shape=(
            jax.ShapeDtypeStruct((LANES, LANES), f32),
            jax.ShapeDtypeStruct((1, ad), f32),
            jax.ShapeDtypeStruct((1, bd), f32),
        ),
        in_specs=[pl.BlockSpec(memory_space=pltpu.VMEM)] * 3,
        out_specs=tuple([pl.BlockSpec(memory_space=pltpu.VMEM)] * 3),
    )(rotation, pa, pb)
    return rotation, pa.reshape(ad), pb.reshape(bd)


def local(table_a, table_b, index_a, index_b, rotation_prev, column_prior):
    na, nb = lax.axis_size("aa"), lax.axis_size("ba")
    ad, bd = index_a.shape[0], index_b.shape[0]
    cols = na * nb * bd
    fits = (
        na % 2 == 0 and nb % 2 == 0 and table_a.shape[1] == LANES
        and ad % PACK == 0 and ad <= LANES and bd % PACK == 0 and LANES % bd == 0
        and cols % LANES == 0 and 4 * na * ad * cols <= SCORE_BYTES
    )
    args = (table_a, table_b, index_a, index_b, rotation_prev, column_prior)
    return local_kernel(na, nb, *args) if fits else local_collectives(*args)


def solution(mesh):
    return jax.shard_map(
        local,
        mesh=mesh,
        in_specs=(
            P(("aa", "ba"), None),
            P(("aa", "ba"), None),
            P(("aa", "ba")),
            P(("aa", "ba")),
            P(),
            P(("aa", "ba")),
        ),
        out_specs=(P(), P(("aa", "ba")), P(("aa", "ba"))),
        check_vma=False,
    )
```
